256 devices in a mesh: blk: 32 (over z_hi, x, core), grp: 8 (over z_lo, y).
Axes of the slice: x: 4, y: 4, z: 8 (z_hi: 4, z_lo: 2; z = z_hi * 2 + z_lo), core: 2. Of those that a mesh axis runs over, the one named last changes fastest.
Arguments:
- inv_tiles: bfloat16 [64, 64, 512, 512], P(None, 'grp', 'blk'), may hold values from -6 to 6
- factor: bfloat16 [8, 16, 512, 512], P('grp', None, 'blk'), may hold values from -0.0625 to 0.0625
- diag_inv_factor: float32 [8, 512, 512], P('grp', 'blk'), may hold values from -6 to 6
- structure: int32 [8, 16], replicated, may hold values from 0 to 63, as said below
Outputs:
- offdiag_inv: bfloat16 [8, 16, 512, 512], P('grp', None, 'blk')
- diag_inv: float32 [8, 512, 512], P('grp', 'blk')
The draws below stay inside these ranges and needn't reach their ends.
Inputs may be any that keep to these rules, and one draw needn't show every extreme that they name: `structure`: each row lists 16 distinct ancestor blocks in ascending order, exactly 2 in each run of 8 blocks that starts at a multiple of 8; block 63 is listed in every row.
All inputs are finite; a program needn't handle non-finite values.
Results may differ from the reference program's by a relative error of at most 0.018.
Values may be sent and summed in bfloat16 or wider, within the bound.
A program may use at most 128 MiB of HBM per device.

```python
import jax
import jax.numpy as jnp
from jax import lax

TS = 512
RB = 16
NB = 64
SN = 8
CB = 8
COLSEL = 2


def draw_structure(key, part):
    group_count = RB // COLSEL
    keys = jax.random.split(jax.random.fold_in(key, 17), SN * group_count)

    def choose(subkey):
        shuffled = jax.random.permutation(subkey, CB)
        return jnp.sort(shuffled[:COLSEL])
    picked = jax.vmap(choose)(keys).reshape(SN, group_count, COLSEL).astype(jnp.int32)
    picked = picked.at[:, group_count - 1, COLSEL - 1].set(CB - 1)
    picked = picked.at[0, 0, 0].set(0)
    offsets = jnp.arange(group_count, dtype=jnp.int32)[None, :, None] * CB
    return (picked + offsets).reshape(SN, RB).astype(jnp.int32)


def shard_levels(own_key, extent, pieces, least, largest):
    factor_of = 1.0
    for dim, blocks in pieces:
        heights = jax.random.uniform(jax.random.fold_in(jax.random.fold_in(own_key, 6), dim), (blocks,), jnp.float32, least / len(pieces), largest / len(pieces))
        factor_of = factor_of * jnp.repeat(jnp.exp(heights), extent[dim] // blocks).reshape((-1,) + (1,) * (len(extent) - 1 - dim))
    return factor_of


def gaussian(stream_key, dims, spread, most, shards=(), held_as=jnp.bfloat16):
    result = jax.random.normal(stream_key, dims, jnp.float32) * spread
    if len(shards) > 0:
        result = shard_levels(stream_key, dims, shards, -0.22, 0.18) * result
    return jnp.clip(result, min=-most, max=most).astype(held_as)


def setup_inputs(seed: int = 0) -> dict:
    splits = jax.random.split(jax.random.key(seed), 5)
    return {
        "inv_tiles": gaussian(splits[0], (NB, NB, TS, TS), 1.0, 6.0, ((1, 8), (2, 32))),
        "factor": gaussian(splits[1], (SN, RB, TS, TS), (TS * RB) ** -0.5, 0.0625, ((0, 8), (2, 32))),
        "diag_inv_factor": gaussian(splits[2], (SN, TS, TS), 1.0, 6.0, ((0, 8), (1, 32)), jnp.float32),
        "structure": draw_structure(jax.random.fold_in(splits[4], 71), 0),
    }


def reference(inv_tiles, factor, diag_inv_factor, structure):
    group_count = RB // COLSEL

    def per_node(packed):
        listed, node_factor, node_diag = packed
        gathered = inv_tiles[listed[:, None], listed[None, :]].astype(jnp.float32)
        gathered = gathered.reshape(RB, group_count, COLSEL, TS, TS)
        grouped = node_factor.astype(jnp.float32).reshape(group_count, COLSEL, TS, TS)
        partial_value = jnp.einsum('igjxy,gjyz->gixz', gathered, grouped)
        partial_value = lax.optimization_barrier(partial_value.astype(jnp.bfloat16)).astype(jnp.float32)
        offdiag = (-jnp.sum(partial_value, axis=0)).astype(jnp.bfloat16)
        correction = jnp.einsum('ixy,ixz->yz', node_factor.astype(jnp.float32), offdiag.astype(jnp.float32))
        return offdiag, node_diag - correction

    offdiag_all, diag_all = lax.map(per_node, (structure, factor, diag_inv_factor))
    return offdiag_all, diag_all
```

```python
import functools

import jax
import jax.numpy as jnp
from jax import lax
from jax.experimental import pallas as pl
from jax.experimental.pallas import tpu as pltpu
from jax.sharding import PartitionSpec as P

MESH = pl.DeviceIdType.MESH
BF16 = jnp.bfloat16
F32 = jnp.float32
NZ, NX, NC, NL, NY = 4, 4, 2, 2, 4
ORDER = [(1, 1), (1, 3), (1, 2), (1, 0), (0, 1), (0, 3), (0, 2), (0, 0)]


def place():
    b = lax.axis_index("blk")
    g = lax.axis_index("grp")
    return b // (NX * NC), (b // NC) % NX, b % NC, g // NY, g % NY


def device(zh, x, c, zl, y):
    return {"blk": (zh * NX + x) * NC + c, "grp": zl * NY + y}


def kernel(
    struct_ref, inv_hbm, fac_hbm, dif_ref, off_ref, diag_ref,
    inv_v, f_v, a_v, b_v, c_snd, c_rcv, c_own, z_snd, z_rcv, o_v, o_rcv,
    g32, g_snd, g_rcv, h_snd, h_rcv,
    ld_sem, f_sem, s1_s, s1_r, zs_s, zs_r, x_s, x_r, w_s, w_r, a_s, a_r,
    fx_s, fx_r, c_s, c_r, q_s, q_r, o_s, o_r, g_s, g_r, h_s, h_r,
):
    zh, x, c, zl, y = place()
    sib = 1 - c
    grp = zl * NY + y
    steps = len(ORDER)
    xr, xl = (x + 1) % NX, (x + NX - 1) % NX

    def remote(src, dst, ssem, rsem, dev):
        return pltpu.make_async_remote_copy(
            src_ref=src, dst_ref=dst, send_sem=ssem, recv_sem=rsem,
            device_id=dev, device_id_type=MESH)

    loads = []
    for n in range(8):
        part = pl.ds(8 * n, 8)
        loads.append(pltpu.make_async_copy(inv_hbm.at[part], inv_v.at[part], ld_sem.at[n]))
    load_f = pltpu.make_async_copy(fac_hbm.at[0], f_v.at[c], f_sem)
    for cp in loads:
        cp.start()
    load_f.start()

    partners = []
    for dl in range(NL):
        for dy in range(NY):
            for dc in range(NC):
                if dl or dy or dc:
                    partners.append(device(zh, x, (c + dc) % NC, (zl + dl) % NL, (y + dy) % NY))
    for dz in range(1, NZ):
        for dc in range(NC):
            partners.append(device((zh + dz) % NZ, x, (c + dc) % NC, zl, y))
    for dx in range(1, NX):
        partners.append(device(zh, (x + dx) % NX, c, zl, y))
    bar = pltpu.get_barrier_semaphore()
    for dev in partners:
        pl.semaphore_signal(bar, inc=1, device_id=dev, device_id_type=MESH)
    pl.semaphore_wait(bar, len(partners))

    sends = []
    local1 = None
    for k, (dl, dy) in enumerate(ORDER):
        tl, ty = (zl + NL - dl) % NL, (y + NY - dy) % NY
        tg = tl * NY + ty
        for dc in range(NC):
            tc = (c + dc) % NC
            src = fac_hbm.at[0, pl.ds(2 * tg, 2), :, pl.ds(pl.multiple_of(tc * 256, 256), 256)]
            dst = b_v.at[k, :, zh, x, c]
            if dl == 0 and dy == 0 and dc == 0:
                local1 = pltpu.make_async_copy(src, dst, s1_r.at[k, dc])
                local1.start()
            else:
                cp = remote(src, dst, s1_s.at[k, dc], s1_r.at[k, dc], device(zh, x, tc, tl, ty))
                cp.start()
                sends.append(cp)

    def owner(k):
        dl, dy = ORDER[k]
        return ((zl + dl) % NL) * NY + (y + dy) % NY

    def gather(k):
        s = owner(k)

        def body(i, _):
            row = struct_ref[s, i]
            for j in range(2):
                col = struct_ref[s, 2 * grp + j] % 8
                a_v[k, j, c, i] = inv_v[row, col]
            return 0

        lax.fori_loop(0, 16, body, 0)
        cp = remote(a_v.at[k, :, c], a_v.at[k, :, c], a_s.at[k], a_r.at[k], device(zh, x, sib, zl, y))
        cp.start()
        sends.append(cp)

    def arrived(ref, sem):
        pltpu.make_async_copy(ref, ref, sem).wait()

    def stage_z(k):
        for dc in range(NC):
            src = (c + dc) % NC
            arrived(b_v.at[k, :, zh, x, src], s1_r.at[k, dc])
        for dz in range(1, NZ):
            blockref = b_v.at[k, :, zh, x]
            cp = remote(blockref, blockref, zs_s.at[k, dz - 1], zs_r.at[k, dz - 1],
                        device((zh + dz) % NZ, x, c, zl, y))
            cp.start()
            sends.append(cp)

    def stage_x(k):
        for dz in range(1, NZ):
            arrived(b_v.at[k, :, (zh + NZ - dz) % NZ, x], zs_r.at[k, dz - 1])
        blockref = b_v.at[k, :, :, x]
        for d, tx in enumerate((xr, xl)):
            cp = remote(blockref, blockref, x_s.at[k, d], x_r.at[k, d], device(zh, tx, c, zl, y))
            cp.start()
            sends.append(cp)

    def stage_w(k):
        for d, (fx, tx) in enumerate(((xl, xr), (xr, xl))):
            arrived(b_v.at[k, :, :, fx], x_r.at[k, d])
            blockref = b_v.at[k, d, :, fx]
            cp = remote(blockref, blockref, w_s.at[k, d], w_r.at[k, d], device(zh, tx, c, zl, y))
            cp.start()
            sends.append(cp)

    def compute(k):
        far = (x + 2) % NX
        for d in range(2):
            arrived(b_v.at[k, d, :, far], w_r.at[k, d])
        arrived(a_v.at[k, :, sib], a_r.at[k])
        dl, dy = ORDER[k]
        rhs = [b_v[k, j].reshape(512, 256) for j in range(2)]
        for r in range(NC):
            acc = jnp.dot(a_v[k, 0, r].reshape(256, 512), rhs[0], preferred_element_type=F32)
            acc += jnp.dot(a_v[k, 1, r].reshape(256, 512), rhs[1], preferred_element_type=F32)
            if dy == 0:
                c_own[pl.ds(256 * r, 256), :] = acc
            else:
                c_snd[k, pl.ds(256 * r, 256), :] = acc.astype(BF16)
        if dy:
            cp = remote(c_snd.at[k], c_rcv.at[dl, dy - 1], c_s.at[k], c_r.at[dl, dy - 1],
                        device(zh, x, c, zl, (y + dy) % NY))
            cp.start()
            sends.append(cp)

    def y_sum(dl, rows):
        total = c_own[rows, :]
        for n in range(NY - 1):
            total += c_rcv[dl, n, rows, :].astype(F32)
        return total

    def pass_on():
        for n in range(NY - 1):
            arrived(c_rcv.at[1, n], c_r.at[1, n])

        def body(n, _):
            rows = pl.ds(pl.multiple_of(n * 64, 64), 64)
            z_snd[rows, :] = y_sum(1, rows).astype(BF16)
            return 0

        lax.fori_loop(0, 8, body, 0)
        cp = remote(z_snd, z_rcv, q_s, q_r, device(zh, x, c, 1 - zl, y))
        cp.start()
        sends.append(cp)

    for t in range(steps + 3):
        if t < steps:
            stage_z(t)
        if 1 <= t <= steps:
            stage_x(t - 1)
        if t == 0:
            for cp in loads:
                cp.wait()
        if t < steps:
            gather(t)
        if t == 3:
            load_f.wait()
            cp = remote(f_v.at[c], f_v.at[c], fx_s, fx_r, device(zh, x, sib, zl, y))
            cp.start()
            sends.append(cp)
        if 2 <= t <= steps + 1:
            stage_w(t - 2)
        if t >= 3:
            if t - 3 == 5:
                pass_on()
            compute(t - 3)

    for n in range(NY - 1):
        arrived(c_rcv.at[0, n], c_r.at[0, n])
    arrived(z_rcv, q_r)

    def finish(n, _):
        rows = pl.ds(pl.multiple_of(n * 64, 64), 64)
        o_v[rows, :] = (-(y_sum(0, rows) + z_rcv[rows, :].astype(F32))).astype(BF16)
        return 0

    lax.fori_loop(0, 8, finish, 0)
    give = o_v.at[pl.ds(pl.multiple_of(sib * 256, 256), 256)]
    cp = remote(give, o_rcv, o_s, o_r, device(zh, x, sib, zl, y))
    cp.start()
    sends.append(cp)

    arrived(f_v.at[sib], fx_r)
    for n in range(2):
        cols = pl.ds(256 * n, 256)
        both = f_v[:, :, :, cols].reshape(512, 256)
        corr = lax.dot_general(both, o_v[...], (((0,), (0,)), ((), ())), preferred_element_type=F32)
        corr = corr.reshape(2, NX, 32, 256)
        g32[pl.ds(2 * n, 2)] = corr
        g_snd[pl.ds(2 * n, 2)] = corr.astype(BF16)
    for dx in range(1, NX):
        tx = (x + dx) % NX
        cp = remote(g_snd.at[:, tx], g_rcv.at[dx - 1], g_s.at[dx - 1], g_r.at[dx - 1],
                    device(zh, tx, c, zl, y))
        cp.start()
        sends.append(cp)
    for dx in range(1, NX):
        arrived(g_rcv.at[dx - 1], g_r.at[dx - 1])
    for n in range(NZ):
        total = g32[n, x]
        for dx in range(1, NX):
            total += g_rcv[dx - 1, n].astype(F32)
        h_snd[n] = total.astype(BF16).reshape(NC, 16, 256)
    for dz in range(NZ):
        tz = (zh + dz) % NZ
        for dc in range(NC):
            tc = (c + dc) % NC
            if dz == 0 and dc == 0:
                continue
            cp = remote(h_snd.at[tz, tc], h_rcv.at[dz, c], h_s.at[dz, dc], h_r.at[dz, dc],
                        device(tz, x, tc, zl, y))
            cp.start()
            sends.append(cp)
    h_rcv[0, c] = h_snd[zh, c]

    arrived(o_rcv, o_r)
    mine = pl.ds(pl.multiple_of(c * 256, 256), 256)
    other = pl.ds(pl.multiple_of(sib * 256, 256), 256)
    off_ref[0, :, :, mine] = o_v[mine, :].reshape(16, 16, 256)
    off_ref[0, :, :, other] = o_rcv[...].reshape(16, 16, 256)

    for dz in range(NZ):
        for dc in range(NC):
            if dz == 0 and dc == 0:
                continue
            arrived(h_rcv.at[dz, (c + dc) % NC], h_r.at[dz, dc])
    for half in range(NC):
        cols = slice(256 * half, 256 * half + 256)
        total = dif_ref[0, :, cols]
        for dz in range(NZ):
            total -= h_rcv[dz, half].astype(F32)
        diag_ref[0, :, cols] = total

    for cp in sends:
        cp.wait_send()


def on_device(inv_tiles, factor, diag_inv_factor, structure):
    vm = pltpu.VMEM
    dma = pltpu.SemaphoreType.DMA
    any_space = pl.BlockSpec(memory_space=pltpu.HBM)
    in_vmem = pl.BlockSpec(memory_space=pltpu.VMEM)
    return pl.pallas_call(
        kernel,
        out_shape=(
            jax.ShapeDtypeStruct((1, 16, 16, 512), BF16),
            jax.ShapeDtypeStruct((1, 16, 512), F32),
        ),
        in_specs=[pl.BlockSpec(memory_space=pltpu.SMEM), any_space, any_space, in_vmem],
        out_specs=(in_vmem, in_vmem),
        scratch_shapes=[
            vm((64, 8, 16, 512), BF16),
            vm((2, 16, 16, 512), BF16),
            vm((8, 2, 2, 16, 16, 512), BF16),
            vm((8, 2, NZ, NX, NC, 16, 256), BF16),
            vm((8, 512, 256), BF16),
            vm((2, NY - 1, 512, 256), BF16),
            vm((512, 256), F32),
            vm((512, 256), BF16),
            vm((512, 256), BF16),
            vm((512, 256), BF16),
            vm((256, 256), BF16),
            vm((NZ, NX, 32, 256), F32),
            vm((NZ, NX, 32, 256), BF16),
            vm((NX - 1, NZ, 32, 256), BF16),
            vm((NZ, NC, 16, 256), BF16),
            vm((NZ, NC, 16, 256), BF16),
            dma((8,)), dma(()),
            dma((8, 2)), dma((8, 2)),
            dma((8, 3)), dma((8, 3)),
            dma((8, 2)), dma((8, 2)),
            dma((8, 2)), dma((8, 2)),
            dma((8,)), dma((8,)),
            dma(()), dma(()),
            dma((8,)), dma((2, 3)),
            dma(()), dma(()),
            dma(()), dma(()),
            dma((3,)), dma((3,)),
            dma((4, 2)), dma((4, 2)),
        ],
        compiler_params=pltpu.CompilerParams(
            collective_id=0, has_side_effects=True, vmem_limit_bytes=48 << 20
        ),
    )(structure, inv_tiles, factor, diag_inv_factor)


def solution(mesh):
    return jax.shard_map(
        on_device,
        mesh=mesh,
        in_specs=(
            P(None, "grp", "blk", None),
            P("grp", None, "blk", None),
            P("grp", "blk", None),
            P(),
        ),
        out_specs=(P("grp", None, "blk", None), P("grp", "blk", None)),
        check_vma=False,
    )
```

```python
import jax
import jax.numpy as jnp
from jax import lax
from jax.experimental import pallas as pl
from jax.experimental.pallas import tpu as pltpu
from jax.sharding import PartitionSpec as P

MESH = pl.DeviceIdType.MESH
BF16 = jnp.bfloat16
F32 = jnp.float32
NZ, NX, NC, NL, NY = 4, 4, 2, 2, 4
SLOTS = [(1, 0), (1, 2), (1, 1), (1, 3), (0, 2), (0, 1), (0, 3), (0, 0)]
OWN = 7
STEPS = [(k, 1, 0, 256) for k in range(5)] + [(5, 2, 0, 128), (5, 2, 128, 128), (OWN, 1, 0, 128), (OWN, 1, 128, 128)]
DIRECT = (8,)


def place():
    b = lax.axis_index("blk")
    g = lax.axis_index("grp")
    return b // (NX * NC), (b // NC) % NX, b % NC, g // NY, g % NY


def device(zh, x, c, zl, y):
    return {"blk": (zh * NX + x) * NC + c, "grp": zl * NY + y}


def kernel(
    struct_hbm, inv_hbm, fac_hbm, dif_hbm, off_ref, diag_ref,
    struct_s, inv_v, dif_v, f_v, ft_v, a_v, b_v, c_snd, c_rcv, c_own, z_snd, z_rcv,
    o_v, o_rcv, g32, g_snd, g_rcv, h_snd, h_rcv,
    ld_sem, s1_s, s1_r, zs_s, zs_r, x_s, x_r, w_s, w_r, a_s, a_r,
    fx_s, fx_r, c_s, c_r, q_s, q_r, o_s, o_r, g_s, g_r, h_s, h_r,
):
    zh, x, c, zl, y = place()
    sib = 1 - c
    grp = zl * NY + y
    xr, xl, far = (x + 1) % NX, (x + NX - 1) % NX, (x + 2) % NX
    sends = []
    clock = [0]

    def send(src, dst, ssem, rsem, dev):
        cp = pltpu.make_async_remote_copy(
            src_ref=src, dst_ref=dst, send_sem=ssem, recv_sem=rsem,
            device_id=dev, device_id_type=MESH)
        cp.start()
        sends.append((clock[0], cp))

    def settle(age):
        while sends and clock[0] - sends[0][0] >= age:
            sends.pop(0)[1].wait_send()

    def arrived(ref, sem):
        pltpu.make_async_copy(ref, ref, sem).wait()

    loads = [pltpu.make_async_copy(struct_hbm, struct_s, ld_sem.at[8])]
    for n in range(8):
        part = pl.ds(8 * n, 8)
        loads.append(pltpu.make_async_copy(inv_hbm.at[part], inv_v.at[part], ld_sem.at[n]))
    load_f = pltpu.make_async_copy(fac_hbm.at[0], f_v.at[c], ld_sem.at[9])
    load_d = pltpu.make_async_copy(dif_hbm, dif_v, ld_sem.at[10])

    offsets = [(0, 0, dc, dl, dy) for dl in range(NL) for dy in range(NY) for dc in range(NC)]
    offsets += [(dz, 0, dc, dl, dy) for dz in range(1, NZ) for dc in range(NC) for dl, dy in ((0, 0), SLOTS[0])]
    offsets += [(0, dx, 0, 0, 0) for dx in range(1, NX)]
    partners = [
        device((zh + dz) % NZ, (x + dx) % NX, (c + dc) % NC, (zl + dl) % NL, (y + dy) % NY)
        for dz, dx, dc, dl, dy in offsets if (dz, dx, dc, dl, dy) != (0, 0, 0, 0, 0)
    ]
    bar = pltpu.get_barrier_semaphore()
    for dev in partners:
        pl.semaphore_signal(bar, inc=1, device_id=dev, device_id_type=MESH)
    for cp in loads:
        cp.start()
    load_f.start()
    load_d.start()
    pl.semaphore_wait(bar, len(partners))

    def group_sends(slots, dzs):
        for k in slots:
            dl, dy = SLOTS[k]
            tl, ty = (zl + NL - dl) % NL, (y + NY - dy) % NY
            for dz in dzs:
                for dc in range(NC):
                    tc = (c + dc) % NC
                    src = fac_hbm.at[0, pl.ds(2 * (tl * NY + ty), 2), :, pl.ds(pl.multiple_of(tc * 256, 256), 256)]
                    dst = b_v.at[k, :, zh, x, c]
                    if (dl, dy, dz, dc) == (0, 0, 0, 0):
                        pltpu.make_async_copy(src, dst, s1_r.at[k, dz, dc]).start()
                    else:
                        send(src, dst, s1_s.at[k, dz, dc], s1_r.at[k, dz, dc],
                             device((zh + dz) % NZ, x, tc, tl, ty))

    def gather(k):
        dl, dy = SLOTS[k]
        s = ((zl + dl) % NL) * NY + (y + dy) % NY

        def body(i, _):
            row = struct_s[s, i]
            for j in range(2):
                a_v[k, j, c, i] = inv_v[row, struct_s[s, 2 * grp + j] % 8]
            return 0

        lax.fori_loop(0, 16, body, 0)
        send(a_v.at[k, :, c], a_v.at[k, :, c], a_s.at[k], a_r.at[k], device(zh, x, sib, zl, y))

    def stage_z(k):
        for dc in range(NC):
            arrived(b_v.at[k, :, zh, x, (c + dc) % NC], s1_r.at[k, 0, dc])
        ref = b_v.at[k, :, zh, x]
        for dz in range(1, NZ):
            send(ref, ref, zs_s.at[k, dz - 1], zs_r.at[k, dz - 1], device((zh + dz) % NZ, x, c, zl, y))

    def part(n, j, sz, sx):
        k, many, col, cols = STEPS[n]
        return b_v.at[pl.ds(k, many), j, sz, sx, :, :, pl.ds(col, cols)]

    every = slice(None)

    def stage_x(n):
        k, many, col, cols = STEPS[n]
        if n == 0:
            for dz in range(NZ):
                for dc in range(NC):
                    arrived(b_v.at[k, :, (zh + NZ - dz) % NZ, x, (c + dc) % NC], s1_r.at[k, dz, dc])
        elif col == 0:
            for m in range(k, k + many):
                for dz in range(1, NZ):
                    arrived(b_v.at[m, :, (zh + NZ - dz) % NZ, x], zs_r.at[m, dz - 1])
        ref = part(n, every, every, x)
        for d, tx in enumerate((xr, xl)):
            send(ref, ref, x_s.at[n, d], x_r.at[n, d], device(zh, tx, c, zl, y))
        if n in DIRECT:
            send(ref, ref, w_s.at[n, 0], w_r.at[n, 0], device(zh, far, c, zl, y))

    def stage_w(n):
        for d, (fx, tx) in enumerate(((xl, xr), (xr, xl))):
            arrived(part(n, every, every, fx), x_r.at[n, d])
            if n not in DIRECT:
                ref = part(n, d, every, fx)
                send(ref, ref, w_s.at[n, d], w_r.at[n, d], device(zh, tx, c, zl, y))

    def compute(n):
        k0, many, col, cols = STEPS[n]
        if n in DIRECT:
            arrived(part(n, every, every, far), w_r.at[n, 0])
        else:
            for d in range(2):
                arrived(part(n, d, every, far), w_r.at[n, d])
        lanes = slice(col, col + cols)
        for k in range(k0, k0 + many):
            dl, dy = SLOTS[k]
            if col == 0:
                arrived(a_v.at[k, :, sib], a_r.at[k])
            rhs = [b_v[k, j, :, :, :, :, lanes].reshape(512, cols) for j in range(2)]
            for r in range(NC):
                acc = jnp.dot(a_v[k, 0, r].reshape(256, 512), rhs[0], preferred_element_type=F32)
                acc += jnp.dot(a_v[k, 1, r].reshape(256, 512), rhs[1], preferred_element_type=F32)
                if dy == 0:
                    c_own[dl, pl.ds(256 * r, 256), lanes] = acc
                else:
                    c_snd[k, pl.ds(256 * r, 256), lanes] = acc.astype(BF16)
            if dy:
                half = col // 128
                send(c_snd.at[k, :, pl.ds(col, cols)], c_rcv.at[dl, dy - 1, :, pl.ds(col, cols)],
                     c_s.at[k, half], c_r.at[dl, dy - 1, half], device(zh, x, c, zl, (y + dy) % NY))

    def products(dl):
        for k0, many, col, cols in STEPS:
            for k in range(k0, k0 + many):
                if SLOTS[k][0] == dl and SLOTS[k][1]:
                    dy = SLOTS[k][1]
                    arrived(c_rcv.at[dl, dy - 1, :, pl.ds(col, cols)], c_r.at[dl, dy - 1, col // 128])

    def y_sum(dl, rows):
        total = c_own[dl, rows, :]
        for n in range(NY - 1):
            total += c_rcv[dl, n, rows, :].astype(F32)
        return total

    def pass_on():
        products(1)
        for n in range(8):
            rows = pl.ds(n * 64, 64)
            z_snd[rows, :] = y_sum(1, rows).astype(BF16)
        send(z_snd, z_rcv, q_s, q_r, device(zh, x, c, 1 - zl, y))

    def offdiag():
        products(0)
        arrived(z_rcv, q_r)
        for n in range(8):
            rows = pl.ds(n * 64, 64)
            o_v[rows, :] = (-(y_sum(0, rows) + z_rcv[rows, :].astype(F32))).astype(BF16)

    def correct():
        corr = jnp.dot(ft_v[...], o_v[...], preferred_element_type=F32).reshape(NZ, NX, 32, 256)
        g32[...] = corr
        g_snd[...] = corr.astype(BF16)
        for dx in (2, 1, 3):
            tx = (x + dx) % NX
            send(g_snd.at[:, tx], g_rcv.at[dx - 1], g_s.at[dx - 1], g_r.at[dx - 1], device(zh, tx, c, zl, y))
        give = o_v.at[pl.ds(pl.multiple_of(sib * 256, 256), 256)]
        send(give, o_rcv, o_s, o_r, device(zh, x, sib, zl, y))

    def x_sum():
        for dx in range(1, NX):
            arrived(g_rcv.at[dx - 1], g_r.at[dx - 1])
        for dz in (2, 1, 3, 0):
            tz = (zh + dz) % NZ
            total = g32[tz, x]
            for dx in range(1, NX):
                total += g_rcv[dx - 1, tz].astype(F32)
            h_snd[tz] = total.astype(BF16).reshape(NC, 16, 256)
            for dc in range(NC):
                tc = (c + dc) % NC
                if dz or dc:
                    send(h_snd.at[tz, tc], h_rcv.at[dz, c], h_s.at[dz, dc], h_r.at[dz, dc],
                         device(tz, x, tc, zl, y))
        h_rcv[0, c] = h_snd[zh, c]

    def write_off():
        arrived(o_rcv, o_r)
        mine = pl.ds(pl.multiple_of(c * 256, 256), 256)
        other = pl.ds(pl.multiple_of(sib * 256, 256), 256)
        off_ref[0, :, :, mine] = o_v[mine, :].reshape(16, 16, 256)
        off_ref[0, :, :, other] = o_rcv[...].reshape(16, 16, 256)

    def write_diag():
        for dz in range(NZ):
            for dc in range(NC):
                if dz or dc:
                    arrived(h_rcv.at[dz, (c + dc) % NC], h_r.at[dz, dc])
        for half in range(NC):
            cols = pl.ds(256 * half, 256)
            total = dif_v[0, :, cols]
            for dz in range(NZ):
                total -= h_rcv[dz, half].astype(F32)
            diag_ref[0, :, cols] = total

    def transpose_f():
        arrived(f_v.at[sib], fx_r)
        ft_v[...] = f_v[...].reshape(512, 512).T

    group_sends([0], range(NZ))
    group_sends(range(1, 8), [0])
    zs_at = {0: (1, 2), 1: (3,), 2: (4,), 3: (5, 6), 4: (7,)}
    steps = len(STEPS)
    for t in range(steps):
        clock[0] = t
        stage_x(t)
        for k in zs_at.get(t, ()):
            stage_z(k)
        if t == 0:
            for cp in loads:
                cp.wait()
        if t < 8:
            gather(t)
        if t >= 1:
            stage_w(t - 1)
        if t == 5:
            load_f.wait()
            send(f_v.at[c], f_v.at[c], fx_s, fx_r, device(zh, x, sib, zl, y))
        if t == 7:
            transpose_f()
            load_d.wait()
        if t == 7:
            pass_on()
        if t >= 2:
            compute(t - 2)
        settle(4)
    clock[0] = steps
    compute(steps - 2)
    stage_w(steps - 1)
    compute(steps - 1)
    offdiag()
    correct()
    settle(1)
    write_off()
    x_sum()
    write_diag()
    settle(0)


def on_device(inv_tiles, factor, diag_inv_factor, structure):
    vm = pltpu.VMEM
    dma = pltpu.SemaphoreType.DMA
    hbm = pl.BlockSpec(memory_space=pltpu.HBM)
    out = pl.BlockSpec(memory_space=pltpu.VMEM)
    return pl.pallas_call(
        kernel,
        out_shape=(
            jax.ShapeDtypeStruct((1, 16, 16, 512), BF16),
            jax.ShapeDtypeStruct((1, 16, 512), F32),
        ),
        in_specs=[hbm, hbm, hbm, hbm],
        out_specs=(out, out),
        scratch_shapes=[
            pltpu.SMEM((8, 16), jnp.int32),
            vm((64, 8, 16, 512), BF16),
            vm((1, 16, 512), F32),
            vm((2, 16, 16, 512), BF16),
            vm((512, 512), BF16),
            vm((8, 2, NC, 16, 16, 512), BF16),
            vm((8, 2, NZ, NX, NC, 16, 256), BF16),
            vm((7, 512, 256), BF16),
            vm((2, NY - 1, 512, 256), BF16),
            vm((2, 512, 256), F32),
            vm((512, 256), BF16),
            vm((512, 256), BF16),
            vm((512, 256), BF16),
            vm((256, 256), BF16),
            vm((NZ, NX, 32, 256), F32),
            vm((NZ, NX, 32, 256), BF16),
            vm((NX - 1, NZ, 32, 256), BF16),
            vm((NZ, NC, 16, 256), BF16),
            vm((NZ, NC, 16, 256), BF16),
            dma((11,)),
            dma((8, 4, 2)), dma((8, 4, 2)),
            dma((8, 3)), dma((8, 3)),
            dma((9, 2)), dma((9, 2)),
            dma((9, 2)), dma((9, 2)),
            dma((8,)), dma((8,)),
            dma(()), dma(()),
            dma((7, 2)), dma((2, 3, 2)),
            dma(()), dma(()),
            dma(()), dma(()),
            dma((3,)), dma((3,)),
            dma((4, 2)), dma((4, 2)),
        ],
        compiler_params=pltpu.CompilerParams(
            collective_id=0, has_side_effects=True, vmem_limit_bytes=48 << 20
        ),
    )(*[pltpu.with_memory_space_constraint(v, pltpu.HBM)
        for v in (structure, inv_tiles, factor, diag_inv_factor)])


def solution(mesh):
    return jax.shard_map(
        on_device,
        mesh=mesh,
        in_specs=(
            P(None, "grp", "blk", None),
            P("grp", None, "blk", None),
            P("grp", "blk", None),
            P(),
        ),
        out_specs=(P("grp", None, "blk", None), P("grp", "blk", None)),
        check_vma=False,
    )
```

```python
import jax
import jax.numpy as jnp
from jax import lax
from jax.experimental import pallas as pl
from jax.experimental.pallas import tpu as pltpu
from jax.sharding import PartitionSpec as P

MESH = pl.DeviceIdType.MESH
BF16 = jnp.bfloat16
F32 = jnp.float32
NZ, NX, NC, NL, NY = 4, 4, 2, 2, 4
SLOTS = [(1, 0), (1, 2), (1, 1), (1, 3), (0, 2), (0, 1), (0, 3), (0, 0)]
OWN = 7
STEPS = [(k, 1, 0, 256) for k in range(5)] + [(5, 2, 0, 128), (5, 2, 128, 128), (OWN, 1, 0, 128), (OWN, 1, 128, 128)]
DIRECT = (8,)


def place():
    b = lax.axis_index("blk")
    g = lax.axis_index("grp")
    return b // (NX * NC), (b // NC) % NX, b % NC, g // NY, g % NY


def device(zh, x, c, zl, y):
    return {"blk": (zh * NX + x) * NC + c, "grp": zl * NY + y}


def kernel(
    struct_hbm, inv_hbm, fac_hbm, dif_hbm, off_ref, diag_ref,
    struct_s, inv_v, dif_v, f_v, ft_v, a_v, b_v, c_snd, c_rcv, c_own, z_snd, z_rcv,
    o_v, o_rcv, g_snd, g_rcv,
    ld_sem, s1_s, s1_r, zs_s, zs_r, x_s, x_r, w_s, w_r, a_s, a_r,
    fx_s, fx_r, c_s, c_r, q_s, q_r, o_s, o_r, g_s, g_r,
):
    zh, x, c, zl, y = place()
    sib = 1 - c
    grp = zl * NY + y
    xr, xl, far = (x + 1) % NX, (x + NX - 1) % NX, (x + 2) % NX
    sends = []
    clock = [0]

    def send(src, dst, ssem, rsem, dev):
        cp = pltpu.make_async_remote_copy(
            src_ref=src, dst_ref=dst, send_sem=ssem, recv_sem=rsem,
            device_id=dev, device_id_type=MESH)
        cp.start()
        sends.append((clock[0], cp))

    def settle(age):
        while sends and clock[0] - sends[0][0] >= age:
            sends.pop(0)[1].wait_send()

    def arrived(ref, sem):
        pltpu.make_async_copy(ref, ref, sem).wait()

    loads = [pltpu.make_async_copy(struct_hbm, struct_s, ld_sem.at[8])]
    for n in range(8):
        part = pl.ds(8 * n, 8)
        loads.append(pltpu.make_async_copy(inv_hbm.at[part], inv_v.at[part], ld_sem.at[n]))
    load_f = pltpu.make_async_copy(fac_hbm.at[0], f_v.at[c], ld_sem.at[9])
    load_d = pltpu.make_async_copy(dif_hbm, dif_v, ld_sem.at[10])

    offsets = [(0, 0, dc, dl, dy) for dl in range(NL) for dy in range(NY) for dc in range(NC)]
    offsets += [(dz, 0, dc, dl, dy) for dz in range(1, NZ) for dc in range(NC) for dl, dy in ((0, 0), SLOTS[0])]
    offsets += [(0, dx, 0, 0, 0) for dx in range(1, NX)]
    partners = [
        device((zh + dz) % NZ, (x + dx) % NX, (c + dc) % NC, (zl + dl) % NL, (y + dy) % NY)
        for dz, dx, dc, dl, dy in offsets if (dz, dx, dc, dl, dy) != (0, 0, 0, 0, 0)
    ]
    bar = pltpu.get_barrier_semaphore()
    for dev in partners:
        pl.semaphore_signal(bar, inc=1, device_id=dev, device_id_type=MESH)
    for cp in loads:
        cp.start()
    load_f.start()
    load_d.start()
    pl.semaphore_wait(bar, len(partners))

    def group_sends(slots, dzs):
        for k in slots:
            dl, dy = SLOTS[k]
            tl, ty = (zl + NL - dl) % NL, (y + NY - dy) % NY
            for dz in dzs:
                for dc in range(NC):
                    tc = (c + dc) % NC
                    src = fac_hbm.at[0, pl.ds(2 * (tl * NY + ty), 2), :, pl.ds(pl.multiple_of(tc * 256, 256), 256)]
                    dst = b_v.at[k, :, zh, x, c]
                    if (dl, dy, dz, dc) == (0, 0, 0, 0):
                        pltpu.make_async_copy(src, dst, s1_r.at[k, dz, dc]).start()
                    else:
                        send(src, dst, s1_s.at[k, dz, dc], s1_r.at[k, dz, dc],
                             device((zh + dz) % NZ, x, tc, tl, ty))

    def gather(k):
        dl, dy = SLOTS[k]
        s = ((zl + dl) % NL) * NY + (y + dy) % NY

        def body(i, _):
            row = struct_s[s, i]
            for j in range(2):
                a_v[k, j, c, i] = inv_v[row, struct_s[s, 2 * grp + j] % 8]
            return 0

        lax.fori_loop(0, 16, body, 0)
        send(a_v.at[k, :, c], a_v.at[k, :, c], a_s.at[k], a_r.at[k], device(zh, x, sib, zl, y))

    def stage_z(k):
        for dc in range(NC):
            arrived(b_v.at[k, :, zh, x, (c + dc) % NC], s1_r.at[k, 0, dc])
        ref = b_v.at[k, :, zh, x]
        for dz in range(1, NZ):
            send(ref, ref, zs_s.at[k, dz - 1], zs_r.at[k, dz - 1], device((zh + dz) % NZ, x, c, zl, y))

    def part(n, j, sz, sx):
        k, many, col, cols = STEPS[n]
        return b_v.at[pl.ds(k, many), j, sz, sx, :, :, pl.ds(col, cols)]

    every = slice(None)

    def stage_x(n):
        k, many, col, cols = STEPS[n]
        if n == 0:
            for dz in range(NZ):
                for dc in range(NC):
                    arrived(b_v.at[k, :, (zh + NZ - dz) % NZ, x, (c + dc) % NC], s1_r.at[k, dz, dc])
        elif col == 0:
            for m in range(k, k + many):
                for dz in range(1, NZ):
                    arrived(b_v.at[m, :, (zh + NZ - dz) % NZ, x], zs_r.at[m, dz - 1])
        ref = part(n, every, every, x)
        for d, tx in enumerate((xr, xl)):
            send(ref, ref, x_s.at[n, d], x_r.at[n, d], device(zh, tx, c, zl, y))
        if n in DIRECT:
            send(ref, ref, w_s.at[n, 0], w_r.at[n, 0], device(zh, far, c, zl, y))

    def stage_w(n):
        for d, (fx, tx) in enumerate(((xl, xr), (xr, xl))):
            arrived(part(n, every, every, fx), x_r.at[n, d])
            if n not in DIRECT:
                ref = part(n, d, every, fx)
                send(ref, ref, w_s.at[n, d], w_r.at[n, d], device(zh, tx, c, zl, y))

    def compute(n):
        k0, many, col, cols = STEPS[n]
        if n in DIRECT:
            arrived(part(n, every, every, far), w_r.at[n, 0])
        else:
            for d in range(2):
                arrived(part(n, d, every, far), w_r.at[n, d])
        lanes = slice(col, col + cols)
        for k in range(k0, k0 + many):
            dl, dy = SLOTS[k]
            if col == 0:
                arrived(a_v.at[k, :, sib], a_r.at[k])
            rhs = [b_v[k, j, :, :, :, :, lanes].reshape(512, cols) for j in range(2)]
            for r in range(NC):
                acc = jnp.dot(a_v[k, 0, r].reshape(256, 512), rhs[0], preferred_element_type=F32)
                acc += jnp.dot(a_v[k, 1, r].reshape(256, 512), rhs[1], preferred_element_type=F32)
                if dy == 0:
                    c_own[dl, pl.ds(256 * r, 256), lanes] = acc
                else:
                    c_snd[k, pl.ds(256 * r, 256), lanes] = acc.astype(BF16)
            if dy:
                half = col // 128
                send(c_snd.at[k, :, pl.ds(col, cols)], c_rcv.at[dl, dy - 1, :, pl.ds(col, cols)],
                     c_s.at[k, half], c_r.at[dl, dy - 1, half], device(zh, x, c, zl, (y + dy) % NY))

    def products(dl):
        for k0, many, col, cols in STEPS:
            for k in range(k0, k0 + many):
                if SLOTS[k][0] == dl and SLOTS[k][1]:
                    dy = SLOTS[k][1]
                    arrived(c_rcv.at[dl, dy - 1, :, pl.ds(col, cols)], c_r.at[dl, dy - 1, col // 128])

    def y_sum(dl, rows):
        total = c_own[dl, rows, :]
        for n in range(NY - 1):
            total += c_rcv[dl, n, rows, :].astype(F32)
        return total

    def pass_on():
        products(1)
        for n in range(8):
            rows = pl.ds(n * 64, 64)
            z_snd[rows, :] = y_sum(1, rows).astype(BF16)
        send(z_snd, z_rcv, q_s, q_r, device(zh, x, c, 1 - zl, y))

    def offdiag():
        products(0)
        arrived(z_rcv, q_r)
        for n in range(8):
            rows = pl.ds(n * 64, 64)
            o_v[rows, :] = (-(y_sum(0, rows) + z_rcv[rows, :].astype(F32))).astype(BF16)

    def correct():
        corr = jnp.dot(ft_v[...], o_v[...], preferred_element_type=F32)
        g_snd[...] = corr.astype(BF16).reshape(NZ, NX, NC, 16, 256)
        for dz in (2, 1, 3, 0):
            for dx in (2, 1, 3, 0):
                for dc in range(NC):
                    tz, tx, tc = (zh + dz) % NZ, (x + dx) % NX, (c + dc) % NC
                    src, dst = g_snd.at[tz, tx, tc], g_rcv.at[dz, dx, c]
                    if (dz, dx, dc) == (0, 0, 0):
                        pltpu.make_async_copy(src, dst, g_r).start()
                    else:
                        send(src, dst, g_s.at[dz, dx, dc], g_r, device(tz, tx, tc, zl, y))
        give = o_v.at[pl.ds(pl.multiple_of(sib * 256, 256), 256)]
        send(give, o_rcv, o_s, o_r, device(zh, x, sib, zl, y))

    def write_off():
        arrived(o_rcv, o_r)
        mine = pl.ds(pl.multiple_of(c * 256, 256), 256)
        other = pl.ds(pl.multiple_of(sib * 256, 256), 256)
        off_ref[0, :, :, mine] = o_v[mine, :].reshape(16, 16, 256)
        off_ref[0, :, :, other] = o_rcv[...].reshape(16, 16, 256)

    def write_diag():
        arrived(g_rcv, g_r)
        for half in range(NC):
            cols = pl.ds(256 * half, 256)
            total = dif_v[0, :, cols]
            for dz in range(NZ):
                for dx in range(NX):
                    total -= g_rcv[dz, dx, half].astype(F32)
            diag_ref[0, :, cols] = total

    def transpose_f():
        arrived(f_v.at[sib], fx_r)
        ft_v[...] = f_v[...].reshape(512, 512).T

    group_sends([0], range(NZ))
    group_sends(range(1, 8), [0])
    zs_at = {0: (1, 2), 1: (3,), 2: (4,), 3: (5, 6), 4: (7,)}
    steps = len(STEPS)
    for t in range(steps):
        clock[0] = t
        stage_x(t)
        for k in zs_at.get(t, ()):
            stage_z(k)
        if t == 0:
            for cp in loads:
                cp.wait()
        if t < 8:
            gather(t)
        if t >= 1:
            stage_w(t - 1)
        if t == 5:
            load_f.wait()
            send(f_v.at[c], f_v.at[c], fx_s, fx_r, device(zh, x, sib, zl, y))
        if t == 7:
            transpose_f()
            load_d.wait()
        if t == 7:
            pass_on()
        if t >= 2:
            compute(t - 2)
        settle(4)
    clock[0] = steps
    compute(steps - 2)
    stage_w(steps - 1)
    compute(steps - 1)
    offdiag()
    correct()
    settle(1)
    write_off()
    write_diag()
    settle(0)


def on_device(inv_tiles, factor, diag_inv_factor, structure):
    vm = pltpu.VMEM
    dma = pltpu.SemaphoreType.DMA
    hbm = pl.BlockSpec(memory_space=pltpu.HBM)
    out = pl.BlockSpec(memory_space=pltpu.VMEM)
    return pl.pallas_call(
        kernel,
        out_shape=(
            jax.ShapeDtypeStruct((1, 16, 16, 512), BF16),
            jax.ShapeDtypeStruct((1, 16, 512), F32),
        ),
        in_specs=[hbm, hbm, hbm, hbm],
        out_specs=(out, out),
        scratch_shapes=[
            pltpu.SMEM((8, 16), jnp.int32),
            vm((64, 8, 16, 512), BF16),
            vm((1, 16, 512), F32),
            vm((2, 16, 16, 512), BF16),
            vm((512, 512), BF16),
            vm((8, 2, NC, 16, 16, 512), BF16),
            vm((8, 2, NZ, NX, NC, 16, 256), BF16),
            vm((7, 512, 256), BF16),
            vm((2, NY - 1, 512, 256), BF16),
            vm((2, 512, 256), F32),
            vm((512, 256), BF16),
            vm((512, 256), BF16),
            vm((512, 256), BF16),
            vm((256, 256), BF16),
            vm((NZ, NX, NC, 16, 256), BF16),
            vm((NZ, NX, NC, 16, 256), BF16),
            dma((11,)),
            dma((8, 4, 2)), dma((8, 4, 2)),
            dma((8, 3)), dma((8, 3)),
            dma((9, 2)), dma((9, 2)),
            dma((9, 2)), dma((9, 2)),
            dma((8,)), dma((8,)),
            dma(()), dma(()),
            dma((7, 2)), dma((2, 3, 2)),
            dma(()), dma(()),
            dma(()), dma(()),
            dma((NZ, NX, NC)), dma(()),
        ],
        compiler_params=pltpu.CompilerParams(
            collective_id=0, has_side_effects=True, vmem_limit_bytes=48 << 20
        ),
    )(*[pltpu.with_memory_space_constraint(v, pltpu.HBM)
        for v in (structure, inv_tiles, factor, diag_inv_factor)])


def solution(mesh):
    return jax.shard_map(
        on_device,
        mesh=mesh,
        in_specs=(
            P(None, "grp", "blk", None),
            P("grp", None, "blk", None),
            P("grp", "blk", None),
            P(),
        ),
        out_specs=(P("grp", None, "blk", None), P("grp", "blk", None)),
        check_vma=False,
    )
```

```python
import jax
import jax.numpy as jnp
from jax import lax
from jax.experimental import pallas as pl
from jax.experimental.pallas import tpu as pltpu
from jax.sharding import PartitionSpec as P

MESH = pl.DeviceIdType.MESH
ZS = {0: (1,), 1: (2,), 2: (3,), 3: (4,), 4: (5,), 5: (6,), 6: (7,)}
ZFIRST = False
SLATE = ()
GFIRST = True
WLAG = 1
CLAG = 2
BF16 = jnp.bfloat16
F32 = jnp.float32
NZ, NX, NC, NL, NY = 4, 4, 2, 2, 4
SLOTS = [(1, 0), (1, 2), (1, 1), (1, 3), (0, 2), (0, 1), (0, 3), (0, 0)]
OWN = 7
STEPS = [(0, 1, 0, 128), (0, 1, 128, 128)] + [(k, 1, 0, 256) for k in range(1, 5)] + [(5, 2, 0, 128), (5, 2, 128, 128), (OWN, 1, 0, 128), (OWN, 1, 128, 128)]
DIRECT = (9,)


def place():
    b = lax.axis_index("blk")
    g = lax.axis_index("grp")
    return b // (NX * NC), (b // NC) % NX, b % NC, g // NY, g % NY


def device(zh, x, c, zl, y):
    return {"blk": (zh * NX + x) * NC + c, "grp": zl * NY + y}


def kernel(
    struct_hbm, inv_hbm, fac_hbm, dif_hbm, off_ref, diag_ref,
    struct_s, inv_v, dif_v, f_v, ft_v, a_v, b_v, c_snd, c_rcv, c_own, z_snd, z_rcv,
    o_v, o_rcv, g_snd, g_rcv,
    ld_sem, m_s, m_r, s1_s, s1_r, zs_s, zs_r, x_s, x_r, w_s, w_r, a_s, a_r,
    fx_s, fx_r, c_s, c_r, q_s, q_r, o_s, o_r, g_s, g_r,
):
    zh, x, c, zl, y = place()
    sib = 1 - c
    grp = zl * NY + y
    xr, xl, far = (x + 1) % NX, (x + NX - 1) % NX, (x + 2) % NX
    sends = []
    clock = [0]

    def send(src, dst, ssem, rsem, dev):
        cp = pltpu.make_async_remote_copy(
            src_ref=src, dst_ref=dst, send_sem=ssem, recv_sem=rsem,
            device_id=dev, device_id_type=MESH)
        cp.start()
        sends.append((clock[0], cp))

    def settle(age):
        while sends and clock[0] - sends[0][0] >= age:
            sends.pop(0)[1].wait_send()

    def arrived(ref, sem):
        pltpu.make_async_copy(ref, ref, sem).wait()

    loads = [pltpu.make_async_copy(struct_hbm, struct_s, ld_sem.at[8])]
    for n in range(8):
        part = pl.ds(8 * n, 8)
        loads.append(pltpu.make_async_copy(inv_hbm.at[part], inv_v.at[part], ld_sem.at[n]))
    load_f = pltpu.make_async_copy(fac_hbm.at[0], f_v.at[c], ld_sem.at[9])
    load_d = pltpu.make_async_copy(dif_hbm, dif_v, ld_sem.at[10])

    offsets = [(0, 0, dc, dl, dy) for dl in range(NL) for dy in range(1, NY) for dc in range(NC)]
    offsets += [(dz, 0, dc, 1, 0) for dz in range(NZ) for dc in range(NC)]
    offsets += [(0, 1, 0, 0, 0), (0, NX - 1, 0, 0, 0)]
    partners = [
        device((zh + dz) % NZ, (x + dx) % NX, (c + dc) % NC, (zl + dl) % NL, (y + dy) % NY)
        for dz, dx, dc, dl, dy in offsets
    ]
    bar = pltpu.get_barrier_semaphore()
    for dev in partners:
        pl.semaphore_signal(bar, inc=1, device_id=dev, device_id_type=MESH)
    for cp in loads:
        cp.start()
    load_f.start()
    load_d.start()
    pl.semaphore_wait(bar, len(partners))

    def group_sends(slots, dzs):
        for k in slots:
            dl, dy = SLOTS[k]
            tl, ty = (zl + NL - dl) % NL, (y + NY - dy) % NY
            for dz in dzs:
                for dc in range(NC):
                    tc = (c + dc) % NC
                    src = fac_hbm.at[0, pl.ds(2 * (tl * NY + ty), 2), :, pl.ds(pl.multiple_of(tc * 256, 256), 256)]
                    dst = b_v.at[k, :, zh, x, c]
                    if (dl, dy, dz, dc) == (0, 0, 0, 0):
                        pltpu.make_async_copy(src, dst, s1_r.at[k, dz, dc]).start()
                    else:
                        send(src, dst, s1_s.at[k, dz, dc], s1_r.at[k, dz, dc],
                             device((zh + dz) % NZ, x, tc, tl, ty))

    def merged_sends(half):
        dl, dy = SLOTS[0]
        tl, ty = (zl + NL - dl) % NL, (y + NY - dy) % NY
        for dz in range(NZ):
            for dc in range(NC):
                tc = (c + dc) % NC
                cols = pl.ds(pl.multiple_of(tc * 256 + 128 * half, 128), 128)
                send(fac_hbm.at[0, pl.ds(2 * (tl * NY + ty), 2), :, cols],
                     b_v.at[0, :, zh, x, c, :, pl.ds(128 * half, 128)],
                     m_s.at[half, dz, dc], m_r.at[half, dz, dc], device((zh + dz) % NZ, x, tc, tl, ty))

    def gather(k):
        dl, dy = SLOTS[k]
        s = ((zl + dl) % NL) * NY + (y + dy) % NY

        def body(i, _):
            row = struct_s[s, i]
            for j in range(2):
                a_v[k, j, c, i] = inv_v[row, struct_s[s, 2 * grp + j] % 8]
            return 0

        lax.fori_loop(0, 16, body, 0)
        send(a_v.at[k, :, c], a_v.at[k, :, c], a_s.at[k], a_r.at[k], device(zh, x, sib, zl, y))

    def stage_z(k):
        for dc in range(NC):
            arrived(b_v.at[k, :, zh, x, (c + dc) % NC], s1_r.at[k, 0, dc])
        ref = b_v.at[k, :, zh, x]
        for dz in range(1, NZ):
            send(ref, ref, zs_s.at[k, dz - 1], zs_r.at[k, dz - 1], device((zh + dz) % NZ, x, c, zl, y))

    def part(n, j, sz, sx):
        k, many, col, cols = STEPS[n]
        return b_v.at[pl.ds(k, many), j, sz, sx, :, :, pl.ds(col, cols)]

    every = slice(None)

    def stage_x(n):
        k, many, col, cols = STEPS[n]
        if k == 0:
            for dz in range(NZ):
                for dc in range(NC):
                    arrived(b_v.at[0, :, (zh + NZ - dz) % NZ, x, (c + dc) % NC, :, pl.ds(col, 128)],
                            m_r.at[col // 128, dz, dc])
        elif col == 0:
            for m in range(k, k + many):
                for dz in range(1, NZ):
                    arrived(b_v.at[m, :, (zh + NZ - dz) % NZ, x], zs_r.at[m, dz - 1])
        ref = part(n, every, every, x)
        for d, tx in enumerate((xr, xl)):
            send(ref, ref, x_s.at[n, d], x_r.at[n, d], device(zh, tx, c, zl, y))
        if n in DIRECT:
            send(ref, ref, w_s.at[n, 0], w_r.at[n, 0], device(zh, far, c, zl, y))

    def stage_w(n):
        for d, (fx, tx) in enumerate(((xl, xr), (xr, xl))):
            arrived(part(n, every, every, fx), x_r.at[n, d])
            if n not in DIRECT:
                ref = part(n, d, every, fx)
                send(ref, ref, w_s.at[n, d], w_r.at[n, d], device(zh, tx, c, zl, y))

    def compute(n):
        k0, many, col, cols = STEPS[n]
        if n in DIRECT:
            arrived(part(n, every, every, far), w_r.at[n, 0])
        else:
            for d in range(2):
                arrived(part(n, d, every, far), w_r.at[n, d])
        lanes = slice(col, col + cols)
        for k in range(k0, k0 + many):
            dl, dy = SLOTS[k]
            if col == 0:
                arrived(a_v.at[k, :, sib], a_r.at[k])
            rhs = [b_v[k, j, :, :, :, :, lanes].reshape(512, cols) for j in range(2)]
            for r in range(NC):
                acc = jnp.dot(a_v[k, 0, r].reshape(256, 512), rhs[0], preferred_element_type=F32)
                acc += jnp.dot(a_v[k, 1, r].reshape(256, 512), rhs[1], preferred_element_type=F32)
                if dy == 0:
                    c_own[dl, pl.ds(256 * r, 256), lanes] = acc
                else:
                    c_snd[k, pl.ds(256 * r, 256), lanes] = acc.astype(BF16)
            if dy:
                half = col // 128
                send(c_snd.at[k, :, pl.ds(col, cols)], c_rcv.at[dl, dy - 1, :, pl.ds(col, cols)],
                     c_s.at[k, half], c_r.at[dl, dy - 1, half], device(zh, x, c, zl, (y + dy) % NY))

    def products(dl):
        for k0, many, col, cols in STEPS:
            for k in range(k0, k0 + many):
                if SLOTS[k][0] == dl and SLOTS[k][1]:
                    dy = SLOTS[k][1]
                    arrived(c_rcv.at[dl, dy - 1, :, pl.ds(col, cols)], c_r.at[dl, dy - 1, col // 128])

    def y_sum(dl, rows):
        total = c_own[dl, rows, :]
        for n in range(NY - 1):
            total += c_rcv[dl, n, rows, :].astype(F32)
        return total

    def pass_on():
        products(1)
        for n in range(8):
            rows = pl.ds(n * 64, 64)
            z_snd[rows, :] = y_sum(1, rows).astype(BF16)
        send(z_snd, z_rcv, q_s, q_r, device(zh, x, c, 1 - zl, y))

    def offdiag():
        products(0)
        arrived(z_rcv, q_r)
        for n in range(8):
            rows = pl.ds(n * 64, 64)
            o_v[rows, :] = (-(y_sum(0, rows) + z_rcv[rows, :].astype(F32))).astype(BF16)

    def correct():
        corr = jnp.dot(ft_v[...], o_v[...], preferred_element_type=F32)
        g_snd[...] = corr.astype(BF16).reshape(NZ, NX, NC, 16, 256)
        for dz in (2, 1, 3, 0):
            for dx in (2, 1, 3, 0):
                for dc in range(NC):
                    tz, tx, tc = (zh + dz) % NZ, (x + dx) % NX, (c + dc) % NC
                    src, dst = g_snd.at[tz, tx, tc], g_rcv.at[dz, dx, c]
                    if (dz, dx, dc) == (0, 0, 0):
                        pltpu.make_async_copy(src, dst, g_r).start()
                    else:
                        send(src, dst, g_s.at[dz, dx, dc], g_r, device(tz, tx, tc, zl, y))
        give = o_v.at[pl.ds(pl.multiple_of(sib * 256, 256), 256)]
        send(give, o_rcv, o_s, o_r, device(zh, x, sib, zl, y))

    def write_off():
        arrived(o_rcv, o_r)
        mine = pl.ds(pl.multiple_of(c * 256, 256), 256)
        other = pl.ds(pl.multiple_of(sib * 256, 256), 256)
        off_ref[0, :, :, mine] = o_v[mine, :].reshape(16, 16, 256)
        off_ref[0, :, :, other] = o_rcv[...].reshape(16, 16, 256)

    def write_diag():
        arrived(g_rcv, g_r)
        for half in range(NC):
            cols = pl.ds(256 * half, 256)
            total = dif_v[0, :, cols]
            for dz in range(NZ):
                for dx in range(NX):
                    total -= g_rcv[dz, dx, half].astype(F32)
            diag_ref[0, :, cols] = total

    def transpose_f():
        arrived(f_v.at[sib], fx_r)
        ft_v[...] = f_v[...].reshape(512, 512).T

    merged_sends(0)
    merged_sends(1)
    group_sends([k for k in range(1, OWN) if k not in SLATE], [0])
    steps = len(STEPS)
    done_w, done_c = 0, 0
    for t in range(steps):
        clock[0] = t
        if ZFIRST:
            for k in ZS.get(t, ()):
                stage_z(k)
        stage_x(t)
        if not ZFIRST:
            for k in ZS.get(t, ()):
                stage_z(k)
        if t == 0:
            group_sends([*SLATE, OWN], [0])
            for cp in loads:
                cp.wait()
        if GFIRST and t < 8:
            gather(t)
        if t >= WLAG:
            stage_w(t - WLAG)
        if not GFIRST and t < 8:
            gather(t)
        if t == 5:
            load_f.wait()
            send(f_v.at[c], f_v.at[c], fx_s, fx_r, device(zh, x, sib, zl, y))
        if t == 7:
            transpose_f()
            load_d.wait()
        if t - CLAG == 6:
            pass_on()
        if t >= CLAG:
            compute(t - CLAG)
        settle(4)
    clock[0] = steps
    for n in range(steps - CLAG, steps):
        if WLAG == 2 and n == steps - 3:
            stage_w(steps - 2)
        if n == steps - 1:
            stage_w(steps - 1)
        compute(n)
    offdiag()
    correct()
    settle(1)
    write_off()
    write_diag()
    settle(0)


def on_device(inv_tiles, factor, diag_inv_factor, structure):
    vm = pltpu.VMEM
    dma = pltpu.SemaphoreType.DMA
    hbm = pl.BlockSpec(memory_space=pltpu.HBM)
    out = pl.BlockSpec(memory_space=pltpu.VMEM)
    return pl.pallas_call(
        kernel,
        out_shape=(
            jax.ShapeDtypeStruct((1, 16, 16, 512), BF16),
            jax.ShapeDtypeStruct((1, 16, 512), F32),
        ),
        in_specs=[hbm, hbm, hbm, hbm],
        out_specs=(out, out),
        scratch_shapes=[
            pltpu.SMEM((8, 16), jnp.int32),
            vm((64, 8, 16, 512), BF16),
            vm((1, 16, 512), F32),
            vm((2, 16, 16, 512), BF16),
            vm((512, 512), BF16),
            vm((8, 2, NC, 16, 16, 512), BF16),
            vm((8, 2, NZ, NX, NC, 16, 256), BF16),
            vm((7, 512, 256), BF16),
            vm((2, NY - 1, 512, 256), BF16),
            vm((2, 512, 256), F32),
            vm((512, 256), BF16),
            vm((512, 256), BF16),
            vm((512, 256), BF16),
            vm((256, 256), BF16),
            vm((NZ, NX, NC, 16, 256), BF16),
            vm((NZ, NX, NC, 16, 256), BF16),
            dma((11,)),
            dma((2, 4, 2)), dma((2, 4, 2)),
            dma((8, 4, 2)), dma((8, 4, 2)),
            dma((8, 3)), dma((8, 3)),
            dma((10, 2)), dma((10, 2)),
            dma((10, 2)), dma((10, 2)),
            dma((8,)), dma((8,)),
            dma(()), dma(()),
            dma((7, 2)), dma((2, 3, 2)),
            dma(()), dma(()),
            dma(()), dma(()),
            dma((NZ, NX, NC)), dma(()),
        ],
        compiler_params=pltpu.CompilerParams(
            collective_id=0, has_side_effects=True, vmem_limit_bytes=48 << 20
        ),
    )(*[pltpu.with_memory_space_constraint(v, pltpu.HBM)
        for v in (structure, inv_tiles, factor, diag_inv_factor)])


def solution(mesh):
    return jax.shard_map(
        on_device,
        mesh=mesh,
        in_specs=(
            P(None, "grp", "blk", None),
            P("grp", None, "blk", None),
            P("grp", "blk", None),
            P(),
        ),
        out_specs=(P("grp", None, "blk", None), P("grp", "blk", None)),
        check_vma=False,
    )
```
